32 devices in a mesh: dp: 8 (over z, y), tensor: 4 (over x, core).
Axes of the slice: x: 2, y: 2, z: 4, core: 2. Of those that a mesh axis runs over, the one named last changes fastest.
Arguments:
- patches: bfloat16 [64, 196, 768], P('dp'), may hold values from -6 to 6
- labels: int32 [64], P('dp'), may hold values from 0 to 21842
- image_mask: int32 [64], P('dp'), may hold values from 0 to 1
- patch_weight: float32 [768, 1024], P(('dp', 'tensor')), may hold values from -0.21875 to 0.21875
- attention_weight: float32 [4, 1024, 1024], P(None, 'dp', 'tensor')
- dense_weight: float32 [2, 1024, 4096], P(None, 'dp', 'tensor'), may hold values from -0.1875 to 0.1875
- table_weight: float32 [204, 1024], P(None, 'dp'), may hold values from -3 to 3
- head_weight: float32 [22016, 1024], P(('dp', 'tensor')), may hold values from -3 to 3
- patch_mean: float32 [768, 1024], P(('dp', 'tensor')), may hold values from -0.06 to 0.06
- attention_mean: float32 [4, 1024, 1024], P(None, 'dp', 'tensor'), may hold values from -0.06 to 0.06
- dense_mean: float32 [2, 1024, 4096], P(None, 'dp', 'tensor'), may hold values from -0.06 to 0.06
- table_mean: float32 [204, 1024], P(None, 'dp'), may hold values from -0.06 to 0.06
- head_mean: float32 [22016, 1024], P(('dp', 'tensor')), may hold values from -0.06 to 0.06
- patch_square: float32 [768, 1024], P(('dp', 'tensor')), may hold values from 1e-05 to 0.0001
- attention_square: float32 [4, 1024, 1024], P(None, 'dp', 'tensor'), may hold values from 1e-05 to 0.0001
- dense_square: float32 [2, 1024, 4096], P(None, 'dp', 'tensor'), may hold values from 1e-05 to 0.0001
- table_square: float32 [204, 1024], P(None, 'dp'), may hold values from 1e-05 to 0.0001
- head_square: float32 [22016, 1024], P(('dp', 'tensor')), may hold values from 1e-05 to 0.0001
Outputs:
- patch_master: float32 [768, 1024], P(('dp', 'tensor'))
- attention_master: float32 [4, 1024, 1024], P(None, 'dp', 'tensor')
- dense_master: float32 [2, 1024, 4096], P(None, 'dp', 'tensor')
- table_master: float32 [204, 1024], P(None, 'dp')
- head_master: float32 [22016, 1024], P(('dp', 'tensor'))
- patch_drift: float32 [768, 1024], P(('dp', 'tensor'))
- attention_drift: float32 [4, 1024, 1024], P(None, 'dp', 'tensor')
- dense_drift: float32 [2, 1024, 4096], P(None, 'dp', 'tensor')
- table_drift: float32 [204, 1024], P(None, 'dp')
- head_drift: float32 [22016, 1024], P(('dp', 'tensor'))
- patch_energy: float32 [768, 1024], P(('dp', 'tensor'))
- attention_energy: float32 [4, 1024, 1024], P(None, 'dp', 'tensor')
- dense_energy: float32 [2, 1024, 4096], P(None, 'dp', 'tensor')
- table_energy: float32 [204, 1024], P(None, 'dp')
- head_energy: float32 [22016, 1024], P(('dp', 'tensor'))
- patch_copy: bfloat16 [768, 1024], P(('dp', 'tensor'))
- attention_copy: bfloat16 [4, 1024, 1024], P(None, 'dp', 'tensor')
- dense_copy: bfloat16 [2, 1024, 4096], P(None, 'dp', 'tensor')
- table_copy: bfloat16 [204, 1024], P(None, 'dp')
- head_copy: bfloat16 [22016, 1024], P(('dp', 'tensor'))
- matrix_norms: float32 [9, 2], replicated
- mean_loss: float32 [], replicated
The draws below stay inside these ranges and needn't reach their ends.
Inputs may be any that keep to these rules, and one draw needn't show every extreme that they name: `labels`: labels name real classes.
All inputs are finite; a program needn't handle non-finite values.
Results may differ from the reference program's by a relative error of at most 0.012.
The reference program's roundings to bfloat16 on the way count: a program that leaves them out, or rounds other values in their place, can miss the bound.
Values may be sent and summed in bfloat16 or wider, within the bound.
No kernel may reach another device: no remote copies, remote signals or barrier semaphores. Data moves between devices by JAX's collectives and lax.ppermute only.
A program may use at most 192 MiB of HBM per device.

```python
import math
import jax
import jax.numpy as jnp
from jax import lax

D = 1024
HEADS = 16
HEAD_DIM = 64
FF = 4096
PATCH = 768
CLASSES = 21843
PADDED = 22016
NPATCH = 196
IMG_DEV = 8
SEQ = 197
TAB = 204
IMAGES = 64
N_DP = 8


def draw_attention_weight(key, part):
    base = jax.random.normal(key, (4, D, D), jnp.float32)
    scales = jnp.array([1.0, 1.0, 1.0, 4.0], jnp.float32).reshape(4, 1, 1)
    return base * scales * D ** (-0.5)


def draw_head_weight(key, part):
    base_key = jax.random.fold_in(key, 11)
    common_key = jax.random.fold_in(key, 23)
    base = jnp.clip(jax.random.normal(base_key, (PADDED, D), jnp.float32), -4.0, 4.0)
    common = jnp.clip(jax.random.normal(common_key, (D,), jnp.float32), -3.0, 3.0) * 4.0
    factor = 0.5 + jnp.arange(PADDED, dtype=jnp.float32) / PADDED
    values = (base + factor[:, None] * common[None, :]) * D ** (-0.5)
    return jnp.clip(values, -3.0, 3.0)


def draw_image_mask(key, part):
    draws = jax.random.randint(key, (IMAGES,), 0, 4)
    marks = jnp.where(draws > 0, 1, 0).astype(jnp.int32)
    return marks.at[0].set(1)


def touch_ends(values, key, least, largest):
    spot = [jax.random.randint(jax.random.fold_in(key, axis), (), 0, length) for axis, length in enumerate(values.shape)]
    widest = values.shape.index(max(values.shape))
    beside = spot[:widest] + [(spot[widest] + 1) % values.shape[widest]] + spot[widest + 1:]
    return values.at[tuple(spot)].set(least).at[tuple(beside)].set(largest)


def steps_of(stream_key, shape, cuts, smallest, largest):
    def one(position, shards_of):
        steps = jax.random.uniform(jax.random.fold_in(jax.random.fold_in(stream_key, 6), position), (shards_of,), jnp.float32, smallest / len(cuts), largest / len(cuts))
        return jnp.repeat(jnp.exp(steps), shape[position] // shards_of).reshape((-1,) + (1,) * (len(shape) - position - 1))

    loudness = one(*cuts[0])
    for cut in cuts[1:]:
        loudness = loudness * one(*cut)
    return loudness


def scatter_about(own_key, extent, deviation, most, split=(), kind=jnp.bfloat16):
    loudness = steps_of(own_key, extent, split, -0.22, 0.18) if split else 1.0
    drawn = jax.random.normal(own_key, extent, jnp.float32) * deviation * loudness
    return jnp.minimum(jnp.maximum(drawn, -most), most).astype(kind)


def setup_inputs(seed: int = 0) -> dict:
    arg_keys = jax.random.split(jax.random.key(seed), 19)
    return {
        "patches": scatter_about(arg_keys[0], (IMAGES, NPATCH, PATCH), 1.0, 6.0, ((0, 8),)),
        "labels": touch_ends(jax.random.randint(arg_keys[1], (IMAGES,), 0, CLASSES), jax.random.fold_in(arg_keys[1], 1), 0, CLASSES - 1).astype(jnp.int32),
        "image_mask": draw_image_mask(jax.random.fold_in(arg_keys[18], 71), 0),
        "patch_weight": scatter_about(arg_keys[3], (PATCH, D), PATCH ** -0.5, 0.21875, ((0, 32),), jnp.float32),
        "attention_weight": draw_attention_weight(jax.random.fold_in(arg_keys[18], 71), 0),
        "dense_weight": scatter_about(arg_keys[5], (2, D, FF), D ** -0.5, 0.1875, ((1, 8), (2, 4)), jnp.float32),
        "table_weight": scatter_about(arg_keys[6], (TAB, D), 0.5, 3.0, ((1, 8),), jnp.float32),
        "head_weight": draw_head_weight(jax.random.fold_in(arg_keys[18], 71), 0),
        "patch_mean": scatter_about(arg_keys[8], (PATCH, D), 0.01, 0.06, ((0, 32),), jnp.float32),
        "attention_mean": scatter_about(arg_keys[9], (4, D, D), 0.01, 0.06, ((1, 8), (2, 4)), jnp.float32),
        "dense_mean": scatter_about(arg_keys[10], (2, D, FF), 0.01, 0.06, ((1, 8), (2, 4)), jnp.float32),
        "table_mean": scatter_about(arg_keys[11], (TAB, D), 0.01, 0.06, ((1, 8),), jnp.float32),
        "head_mean": scatter_about(arg_keys[12], (PADDED, D), 0.01, 0.06, ((0, 32),), jnp.float32),
        "patch_square": jnp.clip(jnp.exp(math.log(0.0001) - 2.3025851 * jax.random.uniform(arg_keys[13], (PATCH, D), jnp.float32) ** steps_of(arg_keys[13], (PATCH, D), ((0, 32),), -0.2, 0.2)), 9.999999747378752e-06, 0.0001),
        "attention_square": jnp.clip(jnp.exp(math.log(0.0001) - 2.3025851 * jax.random.uniform(arg_keys[14], (4, D, D), jnp.float32) ** steps_of(arg_keys[14], (4, D, D), ((1, 8), (2, 4)), -0.2, 0.2)), 9.999999747378752e-06, 0.0001),
        "dense_square": jnp.clip(jnp.exp(math.log(0.0001) - 2.3025851 * jax.random.uniform(arg_keys[15], (2, D, FF), jnp.float32) ** steps_of(arg_keys[15], (2, D, FF), ((1, 8), (2, 4)), -0.2, 0.2)), 9.999999747378752e-06, 0.0001),
        "table_square": jnp.clip(jnp.exp(math.log(0.0001) - 2.3025851 * jax.random.uniform(arg_keys[16], (TAB, D), jnp.float32) ** steps_of(arg_keys[16], (TAB, D), ((1, 8),), -0.2, 0.2)), 9.999999747378752e-06, 0.0001),
        "head_square": jnp.clip(jnp.exp(math.log(0.0001) - 2.3025851 * jax.random.uniform(arg_keys[17], (PADDED, D), jnp.float32) ** steps_of(arg_keys[17], (PADDED, D), ((0, 32),), -0.2, 0.2)), 9.999999747378752e-06, 0.0001),
    }


@jax.custom_vjp
def low(v):
    return lax.optimization_barrier(v.astype(jnp.bfloat16)).astype(jnp.float32)

@jax.custom_vjp
def low_back(v):
    return v

def low_keep(v):
    return (low(v), None)

def low_pass(kept, grad):
    return (grad,)

def back_keep(v):
    return (v, None)

def back_low(kept, grad):
    return (low(grad),)
low.defvjp(low_keep, low_pass)
low_back.defvjp(back_keep, back_low)
PRECISE = lax.Precision.HIGHEST
NORM_EPS = 1e-06
ADAM_EPS = 1e-06
LEARNING_RATE = 0.5
WEIGHT_DECAY = 0.01
SMOOTHING = 0.1
MASKED_LOGIT = -1e+30

def layer_norm(inputs, gain, shift):
    average = lax.optimization_barrier(jnp.mean(inputs, -1, keepdims=True))
    centered = inputs - average
    variance = lax.optimization_barrier(jnp.mean(centered * centered, -1, keepdims=True))
    return centered * lax.rsqrt(variance + NORM_EPS) * (1.0 + gain) + shift

def image_losses(lowered, pixels, label_row, mask_row):
    patch_low, attention_low, dense_low, table_low, head_low = lowered
    image_count = pixels.shape[0]
    embedded = low_back(jnp.einsum('bnp,pd->bnd', pixels, patch_low, precision=PRECISE))
    positions = table_low[:SEQ]
    class_token = table_low[SEQ]
    first_token = jnp.broadcast_to(class_token, (image_count, 1, D))
    tokens = jnp.concatenate([first_token, embedded], axis=1) + positions
    norm_one = low(layer_norm(tokens, table_low[SEQ + 1], table_low[SEQ + 2]))
    projected = low(low_back(jnp.einsum('bsd,jde->jbse', norm_one, attention_low[:3], precision=PRECISE)))
    heads_view = projected.reshape(3, image_count, SEQ, HEADS, HEAD_DIM)
    scores = low_back(jnp.einsum('bqhe,bkhe->bhqk', heads_view[0], heads_view[1], precision=PRECISE) * HEAD_DIM ** (-0.5))
    shifted = jnp.exp(scores - lax.optimization_barrier(jnp.max(scores, -1, keepdims=True)))
    probs_low = low(shifted / lax.optimization_barrier(jnp.sum(shifted, -1, keepdims=True)))
    mixed = jnp.einsum('bhqk,bkhe->bqhe', probs_low, heads_view[2], precision=PRECISE).reshape(image_count, SEQ, D)
    mixed = low(low_back(mixed))
    attended = low_back(jnp.einsum('bse,de->bsd', mixed, attention_low[3], precision=PRECISE))
    residual_one = tokens + attended
    norm_two = low(layer_norm(residual_one, table_low[SEQ + 3], table_low[SEQ + 4]))
    hidden = low_back(jnp.einsum('bsd,df->bsf', norm_two, dense_low[0], precision=PRECISE))
    activated = low(jax.nn.gelu(hidden, approximate=False))
    dense_out = low_back(jnp.einsum('bsf,df->bsd', activated, dense_low[1], precision=PRECISE))
    residual_two = residual_one + dense_out
    features = low(layer_norm(residual_two[:, 0], table_low[SEQ + 5], table_low[SEQ + 6]))
    logits = low_back(jnp.einsum('bd,cd->bc', features, head_low, precision=PRECISE))
    class_ids = jnp.arange(PADDED, dtype=jnp.int32)
    class_valid = class_ids < CLASSES
    masked = jnp.where(class_valid[None, :], logits, MASKED_LOGIT)
    row_top = lax.optimization_barrier(jnp.max(masked, -1, keepdims=True))
    log_total = row_top[:, 0] + jnp.log(lax.optimization_barrier(jnp.sum(jnp.exp(masked - row_top), -1)))
    target = lax.optimization_barrier(jnp.sum(jnp.where(class_ids[None, :] == label_row[:, None], logits, 0.0), -1))
    spread = lax.optimization_barrier(jnp.sum(jnp.where(class_valid[None, :], logits, 0.0), -1)) / CLASSES
    row_losses = log_total - (1.0 - SMOOTHING) * target - SMOOTHING * spread
    return jnp.sum(jnp.where(mask_row > 0, row_losses, 0.0))

def lamb_step(weight, gradient, mean_old, square_old, axes):
    mean_new = 0.5 * mean_old + 0.5 * gradient
    square_new = 0.5 * square_old + 0.5 * gradient * gradient
    update = mean_new / (jnp.sqrt(square_new) + ADAM_EPS) + WEIGHT_DECAY * weight
    weight_norm = jnp.sqrt(lax.optimization_barrier(jnp.sum(weight * weight, axes, keepdims=True)))
    update_norm = jnp.sqrt(lax.optimization_barrier(jnp.sum(update * update, axes, keepdims=True)))
    master = weight - LEARNING_RATE * (weight_norm / update_norm) * update
    return (master, mean_new, square_new, weight_norm.reshape(-1), update_norm.reshape(-1))

def reference(patches, labels, image_mask, patch_weight, attention_weight, dense_weight, table_weight, head_weight, patch_mean, attention_mean, dense_mean, table_mean, head_mean, patch_square, attention_square, dense_square, table_square, head_square):
    pixels = patches.astype(jnp.float32).reshape(N_DP, IMG_DEV, NPATCH, PATCH)
    label_blocks = labels.reshape(N_DP, IMG_DEV)
    mask_blocks = image_mask.reshape(N_DP, IMG_DEV)
    real_count = jnp.sum((image_mask > 0).astype(jnp.float32))

    def objective(patch_full, attention_full, dense_full, table_full, head_full):
        lowered = (low(patch_full), low(attention_full), low(dense_full), low(table_full), low(head_full))

        def block_step(running, batch):
            return (running + image_losses(lowered, batch[0], batch[1], batch[2]), None)
        summed, unused = lax.scan(jax.checkpoint(block_step), jnp.zeros((), jnp.float32), (pixels, label_blocks, mask_blocks))
        return summed / real_count
    mean_loss, pullback = jax.vjp(objective, patch_weight, attention_weight, dense_weight, table_weight, head_weight)
    gradients = pullback(jnp.ones_like(mean_loss))
    patch_out = lamb_step(patch_weight, gradients[0], patch_mean, patch_square, (0, 1))
    attention_out = lamb_step(attention_weight, gradients[1], attention_mean, attention_square, (1, 2))
    dense_out = lamb_step(dense_weight, gradients[2], dense_mean, dense_square, (1, 2))
    table_out = lamb_step(table_weight, gradients[3], table_mean, table_square, (0, 1))
    head_out = lamb_step(head_weight, gradients[4], head_mean, head_square, (0, 1))
    ordered = (patch_out, head_out, attention_out, dense_out, table_out)
    weight_norms = jnp.concatenate([item[3] for item in ordered])
    update_norms = jnp.concatenate([item[4] for item in ordered])
    matrix_norms = jnp.stack([weight_norms, update_norms], axis=1)
    return (patch_out[0], attention_out[0], dense_out[0], table_out[0], head_out[0], patch_out[1], attention_out[1], dense_out[1], table_out[1], head_out[1], patch_out[2], attention_out[2], dense_out[2], table_out[2], head_out[2], patch_out[0].astype(jnp.bfloat16), attention_out[0].astype(jnp.bfloat16), dense_out[0].astype(jnp.bfloat16), table_out[0].astype(jnp.bfloat16), head_out[0].astype(jnp.bfloat16), matrix_norms, mean_loss)
```

```python
from functools import partial

import jax
import jax.numpy as jnp
from jax import lax
from jax.sharding import PartitionSpec as P

HEADS = 16
HEAD_DIM = 64
CLASSES = 21843

NORM_EPS = 1e-06
ADAM_EPS = 1e-06
LEARNING_RATE = 0.5
WEIGHT_DECAY = 0.01
SMOOTHING = 0.1
MASKED_LOGIT = -1e30


EVERY = ("dp", "tensor")
LOW = jnp.bfloat16
WIDE = jnp.float32


def norm_forward(inputs, gain, shift):
    average = jnp.mean(inputs, -1, keepdims=True)
    centered = inputs - average
    inverse_scale = lax.rsqrt(jnp.mean(centered * centered, -1, keepdims=True) + NORM_EPS)
    normal = centered * inverse_scale
    return (normal * (1.0 + gain) + shift, normal, inverse_scale)


def norm_pull(out_grad, normal, inverse_scale, gain):
    normal_grad = out_grad * (1.0 + gain)
    return inverse_scale * (
        normal_grad
        - jnp.mean(normal_grad, -1, keepdims=True)
        - normal * jnp.mean(normal_grad * normal, -1, keepdims=True)
    )


def lamb_moments(weight, gradient, mean_old, square_old):
    mean_new = 0.5 * mean_old + 0.5 * gradient
    square_new = 0.5 * square_old + 0.5 * gradient * gradient
    update = mean_new / (jnp.sqrt(square_new) + ADAM_EPS) + WEIGHT_DECAY * weight
    return (mean_new, square_new, update)


def exchange(blocks, axis):
    return lax.all_to_all(blocks, axis, 0, 0, tiled=True)


def spread(block, count):
    return jnp.broadcast_to(block[None], (count,) + block.shape)


def swap(slots, axis):
    count = len(slots)
    return [slots[0]] + [
        lax.ppermute(slots[k], axis, [(j, j ^ k) for j in range(count)]) for k in range(1, count)
    ]


def doubling_gather(block, axis, count, rank):
    held, depth, bit = block, 0, count // 2
    while bit:
        other = lax.ppermute(held, axis, [(j, j ^ bit) for j in range(count)])
        upper = (rank & bit) > 0
        held = jnp.stack(
            [jnp.where(upper, other, held), jnp.where(upper, held, other)], axis=depth
        )
        depth, bit = depth + 1, bit // 2
    return held.reshape((count,) + block.shape)


def two_parts(value):
    high = lax.reduce_precision(value, 8, 7)
    return high.astype(LOW), (value - high).astype(LOW)


def three_parts(value):
    high = lax.reduce_precision(value, 8, 7)
    rest = value - high
    middle = lax.reduce_precision(rest, 8, 7)
    return jnp.stack([high, middle, rest - middle]).astype(LOW)


def pad_rows(value, rows):
    return jnp.pad(value, [(0, 0)] * (value.ndim - 2) + [(0, rows - value.shape[-2]), (0, 0)])


def pad_lanes(value, lanes):
    return jnp.pad(value, [(0, 0)] * (value.ndim - 1) + [(0, lanes - value.shape[-1])])


def dots(left, right, contract):
    return lax.dot_general(left, right, (contract, ((), ())), preferred_element_type=WIDE)


def local(
    patches,
    labels,
    image_mask,
    patch_weight,
    attention_weight,
    dense_weight,
    table_weight,
    head_weight,
    patch_mean,
    attention_mean,
    dense_mean,
    table_mean,
    head_mean,
    patch_square,
    attention_square,
    dense_square,
    table_square,
    head_square,
):
    images, patch_count, pixel_count = patches.shape
    tokens = patch_count + 1
    width = patch_weight.shape[1]
    tensors = lax.axis_size("tensor")
    datas = lax.axis_size("dp")
    devices = datas * tensors
    t_rank = lax.axis_index("tensor")
    d_rank = lax.axis_index("dp")
    own = images // tensors
    total = images * datas
    heads_own = HEADS // tensors
    model_own = width // datas
    feature_own = width // tensors
    feature_part = feature_own // datas
    hidden_own = dense_weight.shape[2]
    hidden_part = hidden_own // datas
    half = width // 2
    score_scale = HEAD_DIM ** (-0.5)
    order = t_rank ^ jnp.arange(tensors)
    own_model = d_rank * model_own
    lanes = 128
    lines = width // lanes

    table_bf = table_weight.astype(LOW)
    label_rows = pad_lanes(
        jnp.stack([labels // 256, labels % 256, (image_mask > 0).astype(jnp.int32)]), model_own
    ).astype(LOW)
    few = jnp.concatenate(
        [table_bf[tokens : tokens + 1], table_bf[0:1], table_bf[tokens + 1 : tokens + 3], label_rows], 0
    )
    few = pad_rows(few, 8)
    pair_rows = jnp.swapaxes(attention_weight[:2], 1, 2).astype(LOW)
    pair_rows = pair_rows.reshape(2, datas, feature_part, model_own).swapaxes(0, 1)
    pair_rows = pair_rows.reshape(datas, 2 * feature_part, model_own)
    first = exchange(jnp.concatenate([spread(few, datas), pair_rows], 1), "dp")
    few_all = first[:, :4].swapaxes(0, 1).reshape(4, width).astype(WIDE)
    label_all = first[:, 4:7, :images].astype(jnp.int32)
    all_labels = (label_all[:, 0] * 256 + label_all[:, 1]).reshape(-1)
    all_mask = label_all[:, 2].reshape(-1)
    pair_all = first[:, 8:].reshape(datas, 2, feature_part, model_own)
    pair_all = pair_all.transpose(1, 2, 0, 3).reshape(2, feature_part, width)
    query_rows, key_rows = pair_all[0], pair_all[1]

    patch_bf = patch_weight.astype(LOW)
    rows_each = patch_weight.shape[0]
    halves = jnp.stack([patch_bf[:, :half], patch_bf[:, half:]])
    half_blocks = jnp.broadcast_to(halves[None], (devices // 2, 2, rows_each, half))
    patch_half = exchange(half_blocks.reshape(devices, rows_each, half), EVERY)
    patch_half = patch_half.reshape(pixel_count, half)
    partner = [(j, j ^ 1) for j in range(tensors)]
    patch_other = lax.ppermute(patch_half, "tensor", partner)
    upper = (t_rank % 2) == 1
    patch_low = jnp.concatenate(
        [jnp.where(upper, patch_other, patch_half), jnp.where(upper, patch_half, patch_other)], 1
    )

    class_input = few_all[0] + few_all[1]
    gain_one, shift_one = few_all[2], few_all[3]
    class_norm, class_normal, class_scale = norm_forward(class_input, gain_one, shift_one)
    class_low = class_norm.astype(LOW)
    query_part = dots(class_low[None], query_rows, ((1,), (1,))).astype(LOW)
    key_part = dots(query_part, key_rows, ((1,), (0,)))
    key_all = exchange(spread(key_part.reshape(lines, lanes), devices), EVERY)
    group = datas // heads_own
    key_all = key_all.reshape(heads_own, group, tensors, width).sum(1)
    query_key = key_all.swapaxes(0, 1)
    query_key = jnp.take(query_key, order, axis=0).reshape(HEADS, width) * score_scale

    table_all = doubling_gather(table_bf, "dp", datas, d_rank)
    table_values = table_all.swapaxes(0, 1).reshape(table_bf.shape[0], width).astype(WIDE)
    gains = table_values[tokens + 1 :]
    late_bf = attention_weight[2:].astype(LOW)
    late_all = doubling_gather(late_bf, "dp", datas, d_rank)
    late_all = late_all.swapaxes(0, 1).reshape(2, width, feature_own)
    value_low, output_low = late_all[0], late_all[1]
    dense_bf = dense_weight.astype(LOW).reshape(2, model_own, datas, hidden_part)
    dense_all = exchange(dense_bf.transpose(2, 0, 1, 3), "dp")
    dense_all = dense_all.swapaxes(0, 1).reshape(2, width, hidden_part)
    inner_low, outer_low = dense_all[0], dense_all[1]

    head_low = head_weight.astype(LOW)
    block_rows = head_weight.shape[0]
    class_ids = (d_rank * tensors + t_rank) * block_rows + jnp.arange(block_rows, dtype=jnp.int32)
    class_valid = (class_ids < CLASSES)[None, :]
    target_hits = class_ids[None, :] == all_labels[:, None]
    picks = jnp.concatenate([target_hits, class_valid], 0).astype(LOW)
    picked = dots(picks, head_low, ((1,), (0,))).astype(LOW)
    picked = jnp.concatenate(
        [
            picked[:total].reshape(devices, own * lines, lanes),
            spread(picked[total].reshape(lines, lanes), devices),
        ],
        1,
    )
    picked = exchange(picked, EVERY).astype(WIDE).sum(0)
    label_row = picked[: own * lines].reshape(own, width)
    head_sum = picked[own * lines :].reshape(1, width)

    own_patches = lax.dynamic_slice_in_dim(patches, t_rank * own, own, 0)
    flat_patches = own_patches.reshape(own * patch_count, pixel_count)
    embedded = jnp.dot(flat_patches, patch_low, preferred_element_type=WIDE)
    inputs = embedded.reshape(own, patch_count, width) + table_values[1:tokens]
    norm_one, normal_one, scale_one = norm_forward(inputs, gains[0], gains[1])
    low_one = norm_one.astype(LOW)
    query_key_parts = jnp.concatenate(two_parts(query_key), 0)
    scores = lax.dot_general(
        low_one, query_key_parts, (((2,), (1,)), ((), ())), preferred_element_type=WIDE
    )
    scores = scores[..., :HEADS] + scores[..., HEADS:]
    class_score = jnp.sum(class_low.astype(WIDE) * query_key, -1)
    top = jnp.maximum(jnp.max(scores, 1), class_score)
    shifted = jnp.exp(scores - top[:, None])
    class_shifted = jnp.exp(class_score - top)
    score_sum = jnp.sum(shifted, 1) + class_shifted
    probs = shifted / score_sum[:, None]
    class_probs = class_shifted / score_sum
    probs_low = probs.astype(LOW)
    class_probs_low = class_probs.astype(LOW)
    blend = lax.dot_general(
        probs_low, low_one, (((1,), (1,)), ((0,), (0,))), preferred_element_type=WIDE
    )
    blend = blend + class_probs_low.astype(WIDE)[..., None] * class_low.astype(WIDE)
    blend_low = blend.astype(LOW).reshape(own, tensors, heads_own, width)
    blend_all = jnp.stack(swap([blend_low[:, k] for k in range(tensors)], "tensor"))
    blend_rows = blend_all.reshape(images * heads_own, width)
    head_of = jnp.arange(feature_own) // HEAD_DIM
    head_mask = head_of[None, :] == jnp.arange(heads_own)[:, None]
    mixed = dots(blend_rows, value_low, ((1,), (0,))).reshape(images, heads_own, feature_own)
    mixed_low = jnp.sum(jnp.where(head_mask, mixed, 0.0), 1).astype(LOW)
    attended = dots(mixed_low, output_low, ((1,), (1,))).reshape(tensors, own, width)
    attended = sum(swap([attended[k] for k in range(tensors)], "tensor"))
    residual_one = class_input + attended
    norm_two, normal_two, scale_two = norm_forward(residual_one, gains[2], gains[3])

    low_two = exchange(spread(norm_two.astype(LOW).reshape(own * lines, lanes), devices), EVERY)
    low_two = low_two.reshape(total, width)
    hidden = dots(low_two, inner_low, ((1,), (0,)))
    gelu_low = jax.nn.gelu(hidden, approximate=False).astype(LOW)
    dense_part = dots(gelu_low, outer_low, ((1,), (1,)))
    dense_sum = exchange(dense_part.reshape(devices, own * lines, lanes), EVERY).sum(0)
    residual_two = residual_one + dense_sum.reshape(own, width)
    norm_last, normal_last, scale_last = norm_forward(residual_two, gains[4], gains[5])
    feature_low = norm_last.astype(LOW)

    features = exchange(spread(feature_low.reshape(own * lines, lanes), devices), EVERY)
    features = features.reshape(total, width)
    logits = dots(features, head_low, ((1,), (1,)))
    masked = jnp.where(class_valid, logits, MASKED_LOGIT)
    local_top = jnp.max(masked, -1)
    exps = jnp.where(class_valid, jnp.exp(masked - local_top[:, None]), 0.0)
    local_exp = jnp.sum(exps, -1)
    local_spread = jnp.sum(jnp.where(class_valid, logits, 0.0), -1)
    pulled = dots(exps.astype(LOW), head_low, ((1,), (0,)))
    stats = jnp.stack([local_top, local_exp, local_spread], -1).reshape(devices, 1, own * 3)
    stats = pad_rows(pad_lanes(stats, lanes), 8)
    joined = jnp.concatenate([pulled.reshape(devices, own * lines, lanes), stats], 1)
    joined = exchange(joined, EVERY)
    pulled = joined[:, : own * lines].reshape(devices, own, width)
    stats = joined[:, own * lines, : own * 3].reshape(devices, own, 3)
    row_top = jnp.max(stats[..., 0], 0)
    row_exp = jnp.sum(stats[..., 1] * jnp.exp(stats[..., 0] - row_top), 0)
    row_spread = jnp.sum(stats[..., 2], 0)
    log_total = row_top + jnp.log(row_exp)
    target = jnp.sum(feature_low.astype(WIDE) * label_row, -1)
    real_rows = (all_mask > 0).astype(WIDE)
    real_count = jnp.sum(real_rows)
    own_real = lax.dynamic_slice_in_dim(real_rows, (d_rank * tensors + t_rank) * own, own, 0)
    row_losses = log_total - (1.0 - SMOOTHING) * target - SMOOTHING * row_spread / CLASSES
    loss_part = jnp.sum(own_real * row_losses)
    row_weight = own_real / real_count
    uniform = SMOOTHING / CLASSES
    target_soft = jnp.exp(target - log_total)
    target_grad = lax.reduce_precision(
        row_weight * (target_soft - (1.0 - SMOOTHING) - uniform), 8, 7
    )
    feature_grad = row_weight[:, None] * (
        jnp.sum(jnp.exp(stats[..., 0] - log_total)[..., None] * pulled, 0) - uniform * head_sum
    )
    feature_grad = feature_grad + label_row * (
        target_grad - row_weight * (target_soft - uniform)
    )[:, None]
    grad_two = norm_pull(feature_grad, normal_last, scale_last, gains[4])

    total_row = pad_lanes(three_parts(log_total).reshape(1, 3 * own), lanes)
    back = jnp.concatenate([grad_two.astype(LOW).reshape(own * lines, lanes), pad_rows(total_row, 8)], 0)
    back = exchange(spread(back, devices), EVERY)
    dense_grad_low = back[:, : own * lines].reshape(total, width)
    log_totals = back[:, own * lines, : 3 * own].astype(WIDE).reshape(devices, 3, own).sum(1).reshape(total)
    gelu_grad = dots(dense_grad_low, outer_low, ((1,), (0,)))
    gelu_pull = jax.vjp(partial(jax.nn.gelu, approximate=False), hidden)[1]
    hidden_grad_low = gelu_pull(gelu_grad)[0].astype(LOW)
    norm_two_part = dots(hidden_grad_low, inner_low, ((1,), (1,)))
    norm_two_grad = exchange(norm_two_part.reshape(devices, own * lines, lanes), EVERY).sum(0)
    norm_two_grad = norm_two_grad.reshape(own, width)
    grad_one = grad_two + norm_pull(norm_two_grad, normal_two, scale_two, gains[2])

    out_grad_low = grad_one.astype(LOW)
    out_grads = jnp.stack(swap([out_grad_low] * tensors, "tensor")).reshape(images, width)
    mixed_grad_low = dots(out_grads, output_low, ((1,), (0,))).astype(LOW)
    spread_grad = jnp.where(head_mask[None], mixed_grad_low[:, None], jnp.zeros((), LOW))
    value_pull = dots(spread_grad.reshape(images * heads_own, feature_own), value_low, ((1,), (1,)))
    value_pull = value_pull.astype(LOW).reshape(tensors, own, heads_own, width)
    value_pull = jnp.stack(swap([value_pull[k] for k in range(tensors)], "tensor"), 1)
    value_pull = value_pull.reshape(own, HEADS, width)
    probs_grad = lax.dot_general(
        low_one, value_pull, (((2,), (2,)), ((0,), (0,))), preferred_element_type=WIDE
    )
    class_probs_grad = jnp.sum(value_pull.astype(WIDE) * class_low.astype(WIDE), -1)
    probs_mean = jnp.sum(probs * probs_grad, 1) + class_probs * class_probs_grad
    scores_grad = (probs * (probs_grad - probs_mean[:, None])).astype(LOW)
    class_scores_grad = (class_probs * (class_probs_grad - probs_mean)).astype(LOW).astype(WIDE)
    key_pull = lax.dot_general(
        scores_grad, low_one, (((0, 1), (0, 1)), ((), ())), preferred_element_type=WIDE
    )
    key_pull = key_pull + jnp.sum(class_scores_grad, 0)[:, None] * class_low.astype(WIDE)
    both = jnp.concatenate([scores_grad, scores_grad, probs_low], -1)
    both_rows = jnp.concatenate([spread(query_key_parts, own), value_pull], 1)
    out_grad = lax.dot_general(
        both, both_rows, (((2,), (1,)), ((0,), (0,))), preferred_element_type=WIDE
    )
    class_grad = jnp.sum(
        jnp.sum(class_scores_grad, 0)[:, None] * query_key
        + jnp.sum(class_probs_low.astype(WIDE)[..., None] * value_pull.astype(WIDE), 0),
        0,
    )
    token_grad = norm_pull(out_grad, normal_one, scale_one, gains[0])
    embed_grad = token_grad.astype(LOW).reshape(own * patch_count, width)

    key_dest = jnp.take(key_pull.reshape(tensors, heads_own, width), order, axis=0).swapaxes(0, 1)
    key_dest = jnp.broadcast_to(key_dest[:, None], (heads_own, group, tensors, width))
    key_sum = exchange(key_dest.reshape(devices, lines, lanes), EVERY).sum(0).reshape(1, width)
    query_sum = jnp.sum(key_rows.astype(WIDE) * key_sum, -1) * score_scale
    class_part = class_grad + jnp.sum(query_rows.astype(WIDE) * query_sum[:, None], 0)
    tail = jnp.stack([query_sum, query_part[0].astype(WIDE)]).reshape(1, 2 * feature_part)
    ends = jnp.concatenate(
        [
            jnp.broadcast_to(
                pad_lanes(key_sum.reshape(datas, 1, 1, model_own), lanes), (datas, tensors, 1, lanes)
            ).reshape(devices, 1, lanes),
            spread(pad_lanes(tail, lanes), devices),
        ],
        1,
    )
    last = exchange(
        jnp.concatenate([spread(class_part.reshape(lines, lanes), devices), pad_rows(ends, 8)], 1), EVERY
    )
    class_total = last[:, :lines].sum(0).reshape(width)
    ends = lax.dynamic_index_in_dim(
        last[:, lines : lines + 2].reshape(datas, tensors, 2, lanes), t_rank, 1, keepdims=False
    )
    key_own = ends[::group, 0, :model_own]
    query_own = ends[:, 1, :feature_part].reshape(feature_own)
    query_low_own = ends[:, 1, feature_part : 2 * feature_part].reshape(feature_own)
    class_own = lax.dynamic_slice_in_dim(class_low, own_model, model_own, 0).astype(WIDE)
    query_weight_grad = class_own[:, None] * query_own
    key_weight_grad = (
        jnp.repeat(key_own.T, HEAD_DIM, axis=1) * query_low_own * score_scale
    )

    pieces = jnp.concatenate(
        [
            spread(jnp.concatenate([mixed_low, mixed_grad_low], 1).reshape(-1, model_own), datas),
            out_grads.reshape(images, datas, model_own).swapaxes(0, 1),
            blend_rows.reshape(images * heads_own, datas, model_own).swapaxes(0, 1),
        ],
        1,
    )
    pieces = exchange(pieces, "dp")
    mixed_lines = 2 * images * feature_own // model_own
    mixed_all = pieces[:, :mixed_lines].reshape(total, 2 * feature_own)
    out_all = pieces[:, mixed_lines : mixed_lines + images].reshape(total, model_own)
    blend_own = pieces[:, mixed_lines + images :].reshape(total, heads_own, model_own)
    output_weight_grad = dots(out_all, mixed_all[:, :feature_own], ((0,), (0,)))
    value_weight_grad = jnp.concatenate(
        [
            dots(
                blend_own[:, h],
                mixed_all[:, feature_own + h * HEAD_DIM : feature_own + (h + 1) * HEAD_DIM],
                ((0,), (0,)),
            )
            for h in range(heads_own)
        ],
        1,
    )
    attention_grad = jnp.stack(
        [query_weight_grad, key_weight_grad, value_weight_grad, output_weight_grad]
    )

    units = exchange(spread(jnp.stack([hidden_grad_low, gelu_low]), datas), "dp")
    units = units.transpose(1, 2, 0, 3).reshape(2, total, hidden_own)
    own_two = lax.dynamic_slice_in_dim(low_two, own_model, model_own, 1)
    own_dense = lax.dynamic_slice_in_dim(dense_grad_low, own_model, model_own, 1)
    dense_grad = jnp.stack(
        [dots(own_two, units[0], ((0,), (0,))), dots(own_dense, units[1], ((0,), (0,)))]
    )

    grad_logits = (real_rows / real_count)[:, None] * (
        jnp.where(class_valid, jnp.exp(masked - log_totals[:, None]), 0.0)
        - (1.0 - SMOOTHING) * target_hits.astype(WIDE)
        - uniform * class_valid.astype(WIDE)
    )
    head_grad = dots(grad_logits.astype(LOW), features, ((0,), (0,)))

    pair_patches = lax.dynamic_slice_in_dim(patches, (t_rank // 2) * 2 * own, 2 * own, 0)
    pair_patches = pair_patches.reshape(2 * own * patch_count, pixel_count)
    low_cols, high_cols = embed_grad[:, :half], embed_grad[:, half:]
    sent = lax.ppermute(jnp.where(upper, low_cols, high_cols), "tensor", partner)
    kept = jnp.where(upper, high_cols, low_cols)
    pair_grad = jnp.concatenate([jnp.where(upper, sent, kept), jnp.where(upper, kept, sent)], 0)
    patch_grad = dots(pair_patches, pair_grad, ((0,), (0,)))
    vectors = jnp.stack(
        [
            jnp.sum(out_grad * normal_one, (0, 1)),
            jnp.sum(out_grad, (0, 1)),
            jnp.sum(norm_two_grad * normal_two, 0),
            jnp.sum(norm_two_grad, 0),
            jnp.sum(feature_grad * normal_last, 0),
            jnp.sum(feature_grad, 0),
            jnp.sum(grad_one, 0),
        ]
    )
    table_part = pad_rows(jnp.concatenate([jnp.sum(token_grad, 0), vectors], 0), 256)
    low_rows, high_rows = table_part[:128], table_part[128:]
    table_sent = lax.ppermute(jnp.where(upper, low_rows, high_rows), "tensor", partner)
    table_half = jnp.where(upper, high_rows, low_rows) + table_sent
    table_rows = 128 // tensors
    table_blocks = table_half.reshape(tensors, table_rows, datas, model_own).transpose(2, 0, 1, 3)
    table_blocks = table_blocks.reshape(devices, -1, half).astype(LOW)
    table_lines = table_blocks.shape[1]
    sums = exchange(
        jnp.concatenate(
            [patch_grad.astype(LOW).reshape(devices, rows_each, half), table_blocks], 1
        ),
        EVERY,
    )
    sums = sums.reshape(devices // 2, 2, rows_each + table_lines, half).astype(WIDE).sum(0)
    patch_shard = jnp.concatenate([sums[0, :rows_each], sums[1, :rows_each]], 1)
    table_own = sums[:, rows_each:].reshape(2, table_rows, model_own)
    table_own = jnp.stack(swap([table_own] * tensors, "tensor"))
    table_own = jnp.take(table_own, order, axis=0).swapaxes(0, 1).reshape(256, model_own)
    class_back = norm_pull(class_total, class_normal, class_scale, gain_one)
    class_rows = jnp.stack([class_back, class_total * class_normal, class_total])
    class_rows = lax.dynamic_slice_in_dim(class_rows, own_model, model_own, 1)
    sum_rows = table_own[patch_count : patch_count + 7]
    class_row = class_rows[0:1] + sum_rows[6:7]
    table_shard = jnp.concatenate(
        [
            class_row,
            table_own[:patch_count],
            class_row,
            sum_rows[:2] + class_rows[1:3],
            sum_rows[2:6],
        ],
        0,
    )

    patch_drift, patch_energy, patch_update = lamb_moments(
        patch_weight, patch_shard, patch_mean, patch_square
    )
    head_drift, head_energy, head_update = lamb_moments(
        head_weight, head_grad, head_mean, head_square
    )
    attention_drift, attention_energy, attention_update = lamb_moments(
        attention_weight, attention_grad, attention_mean, attention_square
    )
    dense_drift, dense_energy, dense_update = lamb_moments(
        dense_weight, dense_grad, dense_mean, dense_square
    )
    table_drift, table_energy, table_update = lamb_moments(
        table_weight, table_shard, table_mean, table_square
    )

    def squares(patch, head, attention, dense, table):
        return jnp.concatenate(
            [
                jnp.sum(patch * patch)[None],
                jnp.sum(head * head)[None],
                jnp.sum(attention * attention, (1, 2)),
                jnp.sum(dense * dense, (1, 2)),
                (jnp.sum(table * table) / tensors)[None],
            ]
        )

    square_parts = jnp.concatenate(
        [
            squares(patch_weight, head_weight, attention_weight, dense_weight, table_weight),
            squares(patch_update, head_update, attention_update, dense_update, table_update),
            loss_part[None],
        ]
    )
    square_sums = exchange(spread(pad_lanes(square_parts[None], lanes), devices), EVERY).sum(0)[0]
    matrix_norms = jnp.sqrt(square_sums[:18].reshape(2, 9).T)
    mean_loss = square_sums[18] / real_count
    trust_ratio = LEARNING_RATE * matrix_norms[:, 0] / matrix_norms[:, 1]
    patch_master = patch_weight - trust_ratio[0] * patch_update
    head_master = head_weight - trust_ratio[1] * head_update
    attention_master = attention_weight - trust_ratio[2:6].reshape(4, 1, 1) * attention_update
    dense_master = dense_weight - trust_ratio[6:8].reshape(2, 1, 1) * dense_update
    table_master = table_weight - trust_ratio[8] * table_update
    return (
        patch_master,
        attention_master,
        dense_master,
        table_master,
        head_master,
        patch_drift,
        attention_drift,
        dense_drift,
        table_drift,
        head_drift,
        patch_energy,
        attention_energy,
        dense_energy,
        table_energy,
        head_energy,
        patch_master.astype(jnp.bfloat16),
        attention_master.astype(jnp.bfloat16),
        dense_master.astype(jnp.bfloat16),
        table_master.astype(jnp.bfloat16),
        head_master.astype(jnp.bfloat16),
        matrix_norms,
        mean_loss,
    )


def solution(mesh):
    placed = (
        P("dp", None, None),
        P("dp"),
        P("dp"),
        P(("dp", "tensor"), None),
        P(None, "dp", "tensor"),
        P(None, "dp", "tensor"),
        P(None, "dp"),
        P(("dp", "tensor"), None),
        P(("dp", "tensor"), None),
        P(None, "dp", "tensor"),
        P(None, "dp", "tensor"),
        P(None, "dp"),
        P(("dp", "tensor"), None),
        P(("dp", "tensor"), None),
        P(None, "dp", "tensor"),
        P(None, "dp", "tensor"),
        P(None, "dp"),
        P(("dp", "tensor"), None),
    )
    return jax.shard_map(
        local,
        mesh=mesh,
        in_specs=placed,
        out_specs=(
            P(("dp", "tensor"), None),
            P(None, "dp", "tensor"),
            P(None, "dp", "tensor"),
            P(None, "dp"),
            P(("dp", "tensor"), None),
            P(("dp", "tensor"), None),
            P(None, "dp", "tensor"),
            P(None, "dp", "tensor"),
            P(None, "dp"),
            P(("dp", "tensor"), None),
            P(("dp", "tensor"), None),
            P(None, "dp", "tensor"),
            P(None, "dp", "tensor"),
            P(None, "dp"),
            P(("dp", "tensor"), None),
            P(("dp", "tensor"), None),
            P(None, "dp", "tensor"),
            P(None, "dp", "tensor"),
            P(None, "dp"),
            P(("dp", "tensor"), None),
            P(),
            P(),
        ),
        check_vma=False,
    )
```
